1024 devices in a mesh: dp: 8 (over z_lo, core), blk: 32 (over x, y), head: 4 (over z_hi).
Axes of the slice: x: 4, y: 8, z: 16 (z_hi: 4, z_lo: 4; z = z_hi * 4 + z_lo), core: 2. Of those that a mesh axis runs over, the one named last changes fastest.
Arguments:
- queries: bfloat16 [8, 16384, 4096], P('dp', ('blk', 'head')), may hold values from -8 to 8
- keys: bfloat16 [8, 16384, 512], P('dp', ('blk', 'head')), may hold values from -8 to 8
- values: bfloat16 [8, 16384, 512], P('dp', ('blk', 'head')), may hold values from -6 to 6
- lengths: int32 [8, 48], P('dp'), may hold values from 1 to 1024, 16384 in all within a row
Outputs:
- attended: bfloat16 [8, 16384, 4096], P('dp', ('blk', 'head'))
The draws below stay inside these ranges and needn't reach their ends.
Inputs may be any that keep to these rules, and one draw needn't show every extreme that they name: `lengths`: each row sums to 16384; the longest document has exactly 1024 positions.
All inputs are finite; a program needn't handle non-finite values.
Results may differ from the reference program's by a relative error of at most 0.0035.
Values may be sent and summed in bfloat16 or wider, within the bound.
No kernel may reach another device: no remote copies, remote signals or barrier semaphores. Data moves between devices by JAX's collectives and lax.ppermute only.
A program may use at most 32 MiB of HBM per device.

```python
import math
import jax
import jax.numpy as jnp
import numpy as np
from jax import lax

HEAD_DIM = 128
Q_HEADS = 32
KV_HEADS = 4
NDOC = 48
SEQS = 8
LEN = 16384
BLOCK = 512
DOC_MOST = 1024
REACH = 2
QW = 4096
KW = 512


def draw_queries(key, part):
    base = jnp.clip(jax.random.normal(jax.random.fold_in(key, 1), (SEQS, LEN, QW), jnp.float32), -4.0, 4.0)
    return base.astype(jnp.bfloat16)


def draw_keys(key, part):
    base = jnp.clip(jax.random.normal(jax.random.fold_in(key, 2), (SEQS, LEN, KW), jnp.float32), -4.0, 4.0)
    return base.astype(jnp.bfloat16)


def block_scale(key, shape, split, least, high):
    gain, own = 1.0, jax.random.fold_in(key, 6)
    for axis_at, shards_of in split:
        draws = jnp.exp(jax.random.uniform(jax.random.fold_in(own, axis_at), (shards_of,), jnp.float32, least / len(split), high / len(split)))
        gain = gain * jnp.repeat(draws, shape[axis_at] // shards_of).reshape([-1 if axis == axis_at else 1 for axis in range(len(shape))])
    return gain


def length_profile(amount, total, bound, skew):
    loads = [(1 << 20) // math.isqrt(rank ** skew) + 1 for rank in range(2, amount + 1)]
    spare, given = total - bound - (amount - 1), [1] * (amount - 1)
    while spare > 0:
        movable = [i for i in range(amount - 1) if given[i] < bound]
        whole, budget = sum([loads[i] for i in movable]), spare
        for i in movable:
            more = min(bound - given[i], max(1, budget * loads[i] // whole), spare)
            given[i] = given[i] + more
            spare = spare - more
    return np.array([bound] + given)


def ragged_sizes(key, number_of, total, most, slope):
    if number_of == 2:
        one = jax.random.randint(key, (), max(1, total - most), min(most, total - 1) + 1)
        return jnp.stack([one, total - one])
    tallies = jnp.asarray(length_profile(number_of, total, most, slope), jnp.int32)
    couples = (number_of - 1) // 2
    source_of, receiver = tallies[1:1 + 2 * couples:2], tallies[2:2 + 2 * couples:2]
    slack = jnp.minimum(source_of - 1, most - receiver)
    passed = jax.random.randint(jax.random.fold_in(key, 1), (couples,), 0, 1 << 20) % (slack + 1)
    tallies = tallies.at[1:1 + 2 * couples:2].set(source_of - passed).at[2:2 + 2 * couples:2].set(receiver + passed)
    return tallies[jax.random.permutation(jax.random.fold_in(key, 2), number_of)]


def scatter_about(rng, shape, spread, limit, pieces=(), held_as=jnp.bfloat16):
    values = spread * jax.random.normal(rng, shape, jnp.float32)
    if pieces:
        values = values * block_scale(rng, shape, pieces, -0.22, 0.18)
    return jnp.clip(values, -limit, limit).astype(held_as)


def setup_inputs(seed: int = 0) -> dict:
    seeds = jax.random.split(jax.random.key(seed), 5)
    return {
        "queries": draw_queries(jax.random.fold_in(seeds[4], 71), 0),
        "keys": draw_keys(jax.random.fold_in(seeds[4], 71), 0),
        "values": scatter_about(seeds[2], (SEQS, LEN, KW), 1.0, 6.0, ((0, 8), (1, 128))),
        "lengths": jax.vmap(lambda own: ragged_sizes(own, NDOC, LEN, DOC_MOST, 2))(jax.random.split(seeds[3], SEQS)).reshape((SEQS, NDOC)).astype(jnp.int32),
    }


def one_sequence(operands):
    query_all, key_all, value_all, doc_lengths = operands
    ends = jnp.cumsum(doc_lengths).astype(jnp.int32)
    group = Q_HEADS // KV_HEADS
    front = REACH * BLOCK
    key_pad = jnp.concatenate([jnp.zeros((front, KW), key_all.dtype), key_all], axis=0)
    value_pad = jnp.concatenate([jnp.zeros((front, KW), value_all.dtype), value_all], axis=0)
    count = LEN // BLOCK
    span = (REACH + 1) * BLOCK

    def doc_of(pos):
        return lax.optimization_barrier(jnp.sum((pos[:, None] >= ends[None, :]).astype(jnp.int32), axis=1))

    def one_block(index):
        start = (index * BLOCK).astype(jnp.int32)
        qs = lax.dynamic_slice_in_dim(query_all, start, BLOCK, 0)
        ks = lax.dynamic_slice_in_dim(key_pad, start, span, 0)
        vs = lax.dynamic_slice_in_dim(value_pad, start, span, 0)
        q_pos = start + jnp.arange(BLOCK, dtype=jnp.int32)
        k_pos = start - front + jnp.arange(span, dtype=jnp.int32)
        allowed = (doc_of(q_pos)[:, None] == doc_of(k_pos)[None, :]) & (k_pos[None, :] <= q_pos[:, None]) & (k_pos[None, :] >= 0)
        q4 = qs.reshape(BLOCK, KV_HEADS, group, HEAD_DIM).astype(jnp.float32)
        k3 = ks.reshape(span, KV_HEADS, HEAD_DIM).astype(jnp.float32)
        v3 = vs.reshape(span, KV_HEADS, HEAD_DIM).astype(jnp.float32)
        scores = jnp.einsum('qhgd,khd->hgqk', q4, k3) / jnp.sqrt(jnp.float32(HEAD_DIM))
        scores = jnp.where(allowed, scores, jnp.float32(-1e+30))
        top = lax.optimization_barrier(jnp.max(scores, axis=-1, keepdims=True))
        expo = jnp.exp(scores - top)
        total = lax.optimization_barrier(jnp.sum(expo, axis=-1))
        weight = expo.astype(jnp.bfloat16).astype(jnp.float32)
        summed = jnp.einsum('hgqk,khd->qhgd', weight, v3)
        result = summed / jnp.transpose(total, (2, 0, 1))[..., None]
        return result.reshape(BLOCK, QW).astype(jnp.bfloat16)
    blocks = lax.map(one_block, jnp.arange(count, dtype=jnp.int32))
    return blocks.reshape(LEN, QW)

def reference(queries, keys, values, lengths):
    return lax.map(one_sequence, (queries, keys, values, lengths))
```

```python
import functools
import math

import jax, jax.numpy as jnp
from jax import lax
from jax.experimental import pallas as pl
from jax.experimental.pallas import tpu as pltpu
from jax.sharding import PartitionSpec as P


HEAD_DIM = 128
NEG = -1e30

VMEM_LIMIT = 40 << 20


def doc_starts(lengths, base, rows):
    docs = lengths.shape[1]
    wide = jnp.broadcast_to(lengths.astype(jnp.float32), (docs, docs))
    r = lax.broadcasted_iota(jnp.int32, (docs, docs), 0)
    c = lax.broadcasted_iota(jnp.int32, (docs, docs), 1)
    ends = jnp.sum(jnp.where(c <= r, wide, 0.0), axis=1, keepdims=True)
    pos = (base + lax.broadcasted_iota(jnp.int32, (docs, rows), 1)).astype(jnp.float32)
    ends = jnp.broadcast_to(ends, (docs, rows))
    return jnp.max(jnp.where(ends <= pos, ends, 0.0), axis=0, keepdims=True)


def kernel(spec, chunk, first, last, where_of, group, *refs):
    n = len(spec)
    refs = list(refs)
    lengths_ref, q_ref = refs[0], refs[1]
    ks, vs = refs[2:2 + n], refs[2 + n:2 + 2 * n]
    at = 2 + 2 * n
    if not first:
        acc_in, ml_in = refs[at], refs[at + 1]
        at += 2
    if last:
        o_ref = refs[at]
        at += 1
    else:
        acc_out, ml_out = refs[at], refs[at + 1]
        at += 2
    bias_ref = refs[at]
    rows = q_ref.shape[0]
    base, starts_of = where_of(rows)

    @pl.when(pl.program_id(0) == 0)
    def _():
        start = doc_starts(lengths_ref[...], base, rows)
        key = lax.broadcasted_iota(jnp.int32, (rows, rows), 0)
        query = lax.broadcasted_iota(jnp.int32, (rows, rows), 1)
        for p in range(n):
            ok = (key + starts_of[spec[p]]).astype(jnp.float32) >= start
            if spec[p] == 0:
                ok = ok & (key <= query)
            bias_ref[p] = jnp.where(ok, 0.0, NEG)

    c = math.log2(math.e) / math.sqrt(HEAD_DIM)
    v_turned = jnp.concatenate([v[...].T for v in vs], axis=1)
    for lo in range(0, group, chunk):
        span = slice(lo * HEAD_DIM, (lo + chunk) * HEAD_DIM)
        q = jnp.concatenate([q_ref[:, (lo + t) * HEAD_DIM:(lo + t + 1) * HEAD_DIM] for t in range(chunk)], axis=0)
        scores = []
        for p in range(n):
            s = lax.dot_general(ks[p][...], q, (((1,), (1,)), ((), ())), preferred_element_type=jnp.float32)
            scores.append(s + jnp.concatenate([bias_ref[p]] * chunk, axis=1))
        top = jnp.max(functools.reduce(jnp.maximum, scores), axis=0, keepdims=True)
        if not first:
            before = ml_in[0, 0:1, span]
            top = jnp.maximum(top, before)
        weights = [jnp.exp2((s - top) * c) for s in scores]
        total = jnp.sum(functools.reduce(jnp.add, weights), axis=0, keepdims=True)
        flat = jnp.concatenate([w.astype(jnp.bfloat16) for w in weights], axis=0)
        acc = jnp.dot(v_turned, flat, preferred_element_type=jnp.float32)
        if not first:
            fix = jnp.exp2((before - top) * c)
            total = total + fix * ml_in[0, 1:2, span]
            acc = acc + fix * acc_in[0, :, span]
        if last:
            out = acc / total
            for t in range(chunk):
                o_ref[:, (lo + t) * HEAD_DIM:(lo + t + 1) * HEAD_DIM] = out[:, t * rows:(t + 1) * rows].T.astype(jnp.bfloat16)
        else:
            acc_out[0, :, span] = acc
            ml_out[0, 0:1, span] = top
            ml_out[0, 1:2, span] = total


def attend(lengths, q, pieces, state, last, where_of, chunk=2):
    rows, qw = q.shape
    kv = pieces[0][1].shape[1] // HEAD_DIM
    group = qw // HEAD_DIM // kv
    n = len(pieces)
    spec = [p[0] for p in pieces]

    def at(block):
        return pl.BlockSpec((rows, HEAD_DIM), lambda g: (block, g))

    wide = pl.BlockSpec((rows, group * HEAD_DIM), lambda g: (0, g))
    acc_spec = pl.BlockSpec((1, HEAD_DIM, group * rows), lambda g: (g, 0, 0))
    ml_spec = pl.BlockSpec((1, 2, group * rows), lambda g: (g, 0, 0))
    in_specs = [pl.BlockSpec(lengths.shape, lambda g: (0, 0)), wide]
    in_specs += [at(p[2]) for p in pieces] + [at(p[4]) for p in pieces]
    args = [lengths, q] + [p[1] for p in pieces] + [p[3] for p in pieces]
    if state is not None:
        in_specs += [acc_spec, ml_spec]
        args += list(state)
    if last:
        out_specs, out_shape = wide, jax.ShapeDtypeStruct((rows, qw), jnp.bfloat16)
    else:
        out_specs = [acc_spec, ml_spec]
        out_shape = [
            jax.ShapeDtypeStruct((kv, HEAD_DIM, group * rows), jnp.float32),
            jax.ShapeDtypeStruct((kv, 2, group * rows), jnp.float32),
        ]
    return pl.pallas_call(
        functools.partial(kernel, spec, chunk, state is None, last, where_of, group),
        grid=(kv,),
        in_specs=in_specs,
        out_specs=out_specs,
        out_shape=out_shape,
        scratch_shapes=[pltpu.VMEM((n, rows, rows), jnp.float32)],
        cost_estimate=pl.CostEstimate(
            flops=4 * n * rows * rows * qw,
            bytes_accessed=4 * rows * qw,
            transcendentals=n * rows * rows * qw // HEAD_DIM,
        ),
        compiler_params=pltpu.CompilerParams(vmem_limit_bytes=VMEM_LIMIT),
    )(*args)


NOWHERE = -(1 << 20)


def cycle(value, axis, by):
    count = lax.axis_size(axis)
    return lax.ppermute(value, axis, [(i, (i + by) % count) for i in range(count)])


def onward(value, keep):
    width, cols = lax.axis_size("blk"), lax.axis_size("head")
    pairs = [(b * cols + h, (b + 1) % width * cols + h) for b in range(width) for h in range(cols) if keep(h)]
    return lax.ppermute(value, ("blk", "head"), pairs)


def spread(value, slot):
    width, cols = lax.axis_size("blk"), lax.axis_size("head")
    pairs = []
    for b in range(width):
        for h in range(cols):
            by = 1 if (h + slot) % cols > h else -1
            pairs.append((b * cols + h, (b + by) % width * cols + h))
    return lax.ppermute(value, ("blk", "head"), pairs)


def positions(rows):
    cols = lax.axis_size("head")
    b, h = lax.axis_index("blk"), lax.axis_index("head")

    def first(row, col):
        return (row * cols + col) * rows

    at = {0: first(b, h), 1: first(b - 1, h), 2: first(b - 2, h)}
    for slot in range(1, cols):
        col = lax.rem(h + slot, cols)
        at["same", slot] = jnp.where(col < h, first(b, col), NOWHERE)
        at["one", slot] = first(b - 1, col)
        at["two", slot] = jnp.where(col > h, first(b - 2, col), NOWHERE)
        at["spread", slot] = first(jnp.where(col > h, b - 2, b), col)
    return at[0], at


def on_device(queries, keys, values, lengths):
    q = queries[0]
    own = jnp.concatenate([keys[0], values[0]], axis=0)

    def piece(kind, value):
        return (kind, value, 0, value, 1)

    left = cycle(own, "head", 1)
    right = cycle(own, "head", -1)
    below = cycle(own, "blk", 1)
    across = cycle(below, "head", 2)
    below2 = cycle(below, "blk", 1)
    left1 = cycle(left, "blk", 1)
    right1 = cycle(right, "blk", 1)
    left2 = onward(left1, lambda h: (h + 3) % 4 > h)
    right2 = onward(right1, lambda h: (h + 1) % 4 > h)
    across2 = spread(across, 2)
    first = [piece(0, own), piece(1, below), piece(2, below2), piece(("same", 3), left), piece(("same", 1), right)]
    second = [piece(("one", 3), left1), piece(("one", 1), right1), piece(("one", 2), across)]
    third = [piece(("two", 3), left2), piece(("two", 1), right2), piece(("spread", 2), across2)]
    state = attend(lengths, q, first, None, False, positions, 4)
    state = attend(lengths, q, second, state, False, positions, 4)
    return attend(lengths, q, third, state, True, positions, 4)[None]


def solution(mesh):
    return jax.shard_map(
        on_device,
        mesh=mesh,
        in_specs=(
            P("dp", ("blk", "head"), None),
            P("dp", ("blk", "head"), None),
            P("dp", ("blk", "head"), None),
            P("dp", None),
        ),
        out_specs=P("dp", ("blk", "head"), None),
        check_vma=False,
    )
```

```python
import functools
import math

import jax, jax.numpy as jnp
from jax import lax
from jax.experimental import pallas as pl
from jax.experimental.pallas import tpu as pltpu
from jax.sharding import PartitionSpec as P


HEAD_DIM = 128
NEG = -1e30

VMEM_LIMIT = 40 << 20


def doc_starts(lengths, base, rows):
    docs = lengths.shape[1]
    wide = jnp.broadcast_to(lengths.astype(jnp.float32), (docs, docs))
    r = lax.broadcasted_iota(jnp.int32, (docs, docs), 0)
    c = lax.broadcasted_iota(jnp.int32, (docs, docs), 1)
    ends = jnp.sum(jnp.where(c <= r, wide, 0.0), axis=1, keepdims=True)
    pos = (base + lax.broadcasted_iota(jnp.int32, (docs, rows), 1)).astype(jnp.float32)
    ends = jnp.broadcast_to(ends, (docs, rows))
    return jnp.max(jnp.where(ends <= pos, ends, 0.0), axis=0, keepdims=True)


def kernel(spec, chunk, first, last, where_of, group, *refs):
    n = len(spec)
    refs = list(refs)
    lengths_ref, q_ref = refs[0], refs[1]
    ks, vs = refs[2:2 + n], refs[2 + n:2 + 2 * n]
    at = 2 + 2 * n
    if not first:
        acc_in, ml_in = refs[at], refs[at + 1]
        at += 2
    if last:
        o_ref = refs[at]
        at += 1
    else:
        acc_out, ml_out = refs[at], refs[at + 1]
        at += 2
    bias_ref = refs[at]
    rows = q_ref.shape[0]
    base, starts_of = where_of(rows)

    @pl.when(pl.program_id(0) == 0)
    def _():
        start = doc_starts(lengths_ref[...], base, rows)
        key = lax.broadcasted_iota(jnp.int32, (rows, rows), 0)
        query = lax.broadcasted_iota(jnp.int32, (rows, rows), 1)
        for p in range(n):
            ok = (key + starts_of[spec[p]]).astype(jnp.float32) >= start
            if spec[p] == 0:
                ok = ok & (key <= query)
            bias_ref[p] = jnp.where(ok, 0.0, NEG)

    c = math.log2(math.e) / math.sqrt(HEAD_DIM)
    v_turned = jnp.concatenate([v[...].T for v in vs], axis=1)
    for lo in range(0, group, chunk):
        span = slice(lo * HEAD_DIM, (lo + chunk) * HEAD_DIM)
        q = jnp.concatenate([q_ref[:, (lo + t) * HEAD_DIM:(lo + t + 1) * HEAD_DIM] for t in range(chunk)], axis=0)
        scores = []
        for p in range(n):
            s = lax.dot_general(ks[p][...], q, (((1,), (1,)), ((), ())), preferred_element_type=jnp.float32)
            scores.append(s + jnp.concatenate([bias_ref[p]] * chunk, axis=1))
        top = jnp.max(functools.reduce(jnp.maximum, scores), axis=0, keepdims=True)
        if not first:
            before = ml_in[0, 0:1, span]
            top = jnp.maximum(top, before)
        weights = [jnp.exp2((s - top) * c) for s in scores]
        total = jnp.sum(functools.reduce(jnp.add, weights), axis=0, keepdims=True)
        flat = jnp.concatenate([w.astype(jnp.bfloat16) for w in weights], axis=0)
        acc = jnp.dot(v_turned, flat, preferred_element_type=jnp.float32)
        if not first:
            fix = jnp.exp2((before - top) * c)
            total = total + fix * ml_in[0, 1:2, span]
            acc = acc + fix * acc_in[0, :, span]
        if last:
            out = (acc * (1.0 / total)).astype(jnp.bfloat16)
            for t in range(chunk):
                o_ref[:, (lo + t) * HEAD_DIM:(lo + t + 1) * HEAD_DIM] = out[:, t * rows:(t + 1) * rows].T
        else:
            acc_out[0, :, span] = acc
            ml_out[0, 0:1, span] = top
            ml_out[0, 1:2, span] = total


def attend(lengths, q, pieces, state, last, where_of, chunk=2):
    rows, qw = q.shape
    kv = pieces[0][1].shape[1] // HEAD_DIM
    group = qw // HEAD_DIM // kv
    n = len(pieces)
    spec = [p[0] for p in pieces]

    def at(block):
        return pl.BlockSpec((rows, HEAD_DIM), lambda g: (block, g))

    wide = pl.BlockSpec((rows, group * HEAD_DIM), lambda g: (0, g))
    acc_spec = pl.BlockSpec((1, HEAD_DIM, group * rows), lambda g: (g, 0, 0))
    ml_spec = pl.BlockSpec((1, 2, group * rows), lambda g: (g, 0, 0))
    in_specs = [pl.BlockSpec(lengths.shape, lambda g: (0, 0)), wide]
    in_specs += [at(p[2]) for p in pieces] + [at(p[4]) for p in pieces]
    args = [lengths, q] + [p[1] for p in pieces] + [p[3] for p in pieces]
    if state is not None:
        in_specs += [acc_spec, ml_spec]
        args += list(state)
    if last:
        out_specs, out_shape = wide, jax.ShapeDtypeStruct((rows, qw), jnp.bfloat16)
    else:
        out_specs = [acc_spec, ml_spec]
        out_shape = [
            jax.ShapeDtypeStruct((kv, HEAD_DIM, group * rows), jnp.float32),
            jax.ShapeDtypeStruct((kv, 2, group * rows), jnp.float32),
        ]
    return pl.pallas_call(
        functools.partial(kernel, spec, chunk, state is None, last, where_of, group),
        grid=(kv,),
        in_specs=in_specs,
        out_specs=out_specs,
        out_shape=out_shape,
        scratch_shapes=[pltpu.VMEM((n, rows, rows), jnp.float32)],
        cost_estimate=pl.CostEstimate(
            flops=4 * n * rows * rows * qw,
            bytes_accessed=4 * rows * qw,
            transcendentals=n * rows * rows * qw // HEAD_DIM,
        ),
        compiler_params=pltpu.CompilerParams(vmem_limit_bytes=VMEM_LIMIT),
    )(*args)


NOWHERE = -(1 << 20)


def around(value, by):
    count = lax.axis_size("head")
    return lax.ppermute(value, "head", [(h, (h + by) % count) for h in range(count)])


def onward(value, since, into=lambda h: True):
    width, cols = lax.axis_size("blk"), lax.axis_size("head")
    pairs = [
        ((b - 1) % width * cols + h, b * cols + h)
        for b in range(since, width)
        for h in range(cols)
        if into(h)
    ]
    return lax.ppermute(value, ("blk", "head"), pairs)


def spread(value, by):
    width, cols = lax.axis_size("blk"), lax.axis_size("head")
    pairs = []
    for b in range(width):
        for h in range(cols):
            step = 1 if (h + by) % cols > h else -1
            if step < 0 or b >= 2:
                pairs.append(((b - step) % width * cols + h, b * cols + h))
    return lax.ppermute(value, ("blk", "head"), pairs)


def positions(rows):
    cols = lax.axis_size("head")
    b, h = lax.axis_index("blk"), lax.axis_index("head")

    def first(row, col):
        return (row * cols + col) * rows

    at = {0: first(b, h), 1: first(b - 1, h), 2: first(b - 2, h)}
    for by in range(1, cols):
        col = lax.rem(h + by, cols)
        at["same", by] = jnp.where(col < h, first(b, col), NOWHERE)
        at["one", by] = first(b - 1, col)
        at["two", by] = jnp.where(col > h, first(b - 2, col), NOWHERE)
        at["spread", by] = first(jnp.where(col > h, b - 2, b), col)
    return at[0], at


def on_device(queries, keys, values, lengths):
    q = queries[0]
    own = jnp.concatenate([keys[0], values[0]], axis=0)

    def piece(kind, value):
        return (kind, value, 0, value, 1)

    left = around(own, 1)
    right = around(own, -1)
    below = onward(own, 0)
    across = around(below, 2)
    below2 = onward(below, 2)
    left1 = onward(left, 1)
    right1 = onward(right, 1)
    left2 = onward(left1, 2, lambda h: (h + 3) % 4 > h)
    right2 = onward(right1, 2, lambda h: (h + 1) % 4 > h)
    across2 = spread(across, 2)
    parts = (
        ("ka", [piece(0, own), piece(1, below), piece(2, below2), piece(("same", 3), left)]),
        ("km", [piece(("same", 1), right), piece(("one", 3), left1), piece(("one", 1), right1), piece(("one", 2), across), piece(("two", 3), left2)]),
        ("kt", [piece(("two", 1), right2), piece(("spread", 2), across2)]),
    )
    state = None
    for name, pieces in parts:
        state = attend(lengths, q, pieces, state, name == "kt", positions, 8)
    return state[None]


def solution(mesh):
    return jax.shard_map(
        on_device,
        mesh=mesh,
        in_specs=(
            P("dp", ("blk", "head"), None),
            P("dp", ("blk", "head"), None),
            P("dp", ("blk", "head"), None),
            P("dp", None),
        ),
        out_specs=P("dp", ("blk", "head"), None),
        check_vma=False,
    )
```
